512 devices in a mesh: ep: 64 (over x, z, core), tp: 8 (over y).
Axes of the slice: x: 4, y: 8, z: 8, core: 2. Of those that a mesh axis runs over, the one named last changes fastest.
Arguments:
- tokens: bfloat16 [2, 1024, 4096], P(None, 'ep', 'tp'), may hold values from -6 to 6
- routes: int32 [2, 1024, 8], P(None, 'ep'), may hold values from 0 to 63, all different within a row; in each aligned block of 16 rows (0 to 15, 16 to 31, ..., all dimensions but the last counted through in order) at most 4 rows name the same one
- route_weight: float32 [2, 1024, 8], P(None, 'ep'), may hold values from 0.1 to 0.6
- w_gate: bfloat16 [64, 4096, 1024], P('ep', None, 'tp'), may hold values from -0.09375 to 0.09375
- w_up: bfloat16 [64, 4096, 1024], P('ep', None, 'tp'), may hold values from -0.09375 to 0.09375
- w_down: bfloat16 [64, 1024, 4096], P('ep', 'tp'), may hold values from -0.1875 to 0.1875
Outputs:
- mixed: bfloat16 [2, 1024, 4096], P(None, 'ep', 'tp')
The draws below stay inside these ranges and needn't reach their ends.
Inputs may be any that keep to these rules, and one draw needn't show every extreme that they name: `routes`: each row names 8 different experts. In each micro-batch, at most 4 of the rows of one index of ep name one expert, a bound that some of them reach.
All inputs are finite; a program needn't handle non-finite values.
Results may differ from the reference program's by a relative error of at most 0.015.
Values may be sent and summed in bfloat16 or wider, within the bound.
A program may use at most 64 MiB of HBM per device.

```python
import math
import jax
import jax.numpy as jnp
import numpy as np
from jax import lax

D = 4096
FF = 1024
TOP = 8
MB = 2
TOK_DEV = 16
E = 64
TOKENS = 1024
CAP = 4
N_EP = 64
N_TP = 8


def shard_levels(rng, dims, cuts, low, largest):
    loudness = 1.0
    for dim, shards_of in cuts:
        steps = jax.random.uniform(jax.random.fold_in(jax.random.fold_in(rng, 6), dim), (shards_of,), jnp.float32, low / len(cuts), largest / len(cuts))
        loudness = loudness * jnp.repeat(jnp.exp(steps), dims[dim] // shards_of).reshape((-1,) + (1,) * (len(dims) - 1 - dim))
    return loudness


def shared_out(stream_key, own, number, rows, amount, top, reach, lean):
    ranking = jax.random.permutation(stream_key, amount)
    packed, common = portions_of(amount, rows * top, reach, lean, True), portions_of(amount, rows * top, reach, lean, False)
    places = jnp.arange(amount)

    def named(lengths, rotation):
        used = int((lengths > 0).sum())
        fixed = max(1, used // 4)
        passed = fixed + (places - fixed + rotation * (used - fixed)) % max(1, amount - fixed)
        return jnp.zeros((amount,), jnp.int32).at[ranking[jnp.where(places < fixed, places, passed)]].set(jnp.asarray(lengths, jnp.int32))

    lengths = jnp.where(number % 4 == 0, named(packed, number // 4), named(common, number - number // 4 - 1))
    mixed = jax.random.permutation(jax.random.fold_in(own, 3), amount)
    donor, sink = mixed[0:amount // 2 * 2:2], mixed[1:amount // 2 * 2:2]
    slack = jnp.minimum(lengths[donor] - 1, reach - lengths[sink]) // 2
    slack = jnp.where((donor == ranking[0]) | (sink == ranking[0]) | (lengths[sink] == 0), 0, jnp.maximum(slack, 0))
    passed = jax.random.randint(jax.random.fold_in(own, 4), (amount // 2,), 0, 1 << 20) % (slack + 1)
    lengths = lengths.at[donor].add(-passed).at[sink].add(passed)
    items = jnp.searchsorted(jnp.cumsum(lengths), jnp.arange(rows * top), side="right").astype(jnp.int32)
    table = items.reshape(top, rows).T
    table = table[jax.random.permutation(jax.random.fold_in(own, 1), rows)]
    rotation = jax.random.randint(jax.random.fold_in(own, 2), (rows, 1), 0, top)
    return jnp.take_along_axis(table, (jnp.arange(top)[None, :] + rotation) % top, axis=1)


def portions_of(number_of, total, bound, skew, full):
    loads = [(1 << 20) // math.isqrt(standing ** skew) + 1 for standing in range(1, number_of + 1)]
    largest = bound if full else min(bound, max(-(-total // number_of), total * loads[0] // sum(loads)))
    least = 1 if total - largest >= number_of - 1 else 0
    counts, surplus = [largest] + [least] * (number_of - 1), total - largest - least * (number_of - 1)
    while surplus > 0:
        candidates = [i for i in range(1, number_of) if counts[i] < largest] or [i for i in range(1, number_of) if counts[i] < bound]
        pool, left = sum([loads[i] for i in candidates]), surplus
        for i in candidates:
            addition = min(bound - counts[i], max(1, left * loads[i] // pool), surplus)
            counts[i] = counts[i] + addition
            surplus = surplus - addition
    return np.array(counts)


def centred(key, dims, spread, most, shards=(), kind=jnp.bfloat16):
    entries = jax.random.normal(key, dims, jnp.float32) * spread
    if len(shards) > 0:
        entries = shard_levels(key, dims, shards, -0.22, 0.18) * entries
    return jnp.clip(entries, min=-most, max=most).astype(kind)


def setup_inputs(seed: int = 0) -> dict:
    splits = jax.random.split(jax.random.key(seed), 7)
    tokens = centred(splits[0], (MB, TOKENS, D), 1.0, 6.0, ((1, 64), (2, 8)))
    routes_keys = jax.random.split(jax.random.fold_in(splits[1], 1), MB * TOKENS // TOK_DEV)
    routes_turns = jax.random.permutation(jax.random.fold_in(splits[1], 3), MB * TOKENS // TOK_DEV)
    routes = jax.vmap(lambda own, number: shared_out(jax.random.fold_in(splits[1], 2), own, number, TOK_DEV, E, TOP, CAP, 2))(routes_keys, routes_turns).reshape((MB, TOKENS, TOP))
    route_weight = jnp.clip(0.1 + 0.5 * jax.random.uniform(splits[2], (MB, TOKENS, TOP), jnp.float32) ** shard_levels(splits[2], (MB, TOKENS, TOP), ((1, 64),), -0.2, 0.2), 0.1, 0.6)
    w_gate = centred(splits[3], (E, D, FF), D ** -0.5, 0.09375, ((0, 64), (2, 8)))
    w_up = centred(splits[4], (E, D, FF), D ** -0.5, 0.09375, ((0, 64), (2, 8)))
    w_down = centred(splits[5], (E, FF, D), FF ** -0.5, 0.1875, ((0, 64), (1, 8)))
    return {"tokens": tokens, "routes": routes, "route_weight": route_weight, "w_gate": w_gate, "w_up": w_up, "w_down": w_down}


def expert_rows(row_block, gate_weight_table, up_matrix, down_matrix):
    gate_preactivation = jnp.dot(row_block, gate_weight_table, preferred_element_type=jnp.float32)
    up_pre = jnp.dot(row_block, up_matrix, preferred_element_type=jnp.float32)
    hidden = (jax.nn.silu(gate_preactivation) * up_pre).astype(jnp.bfloat16)
    groups = hidden.reshape(row_block.shape[0], N_TP, FF // N_TP).astype(jnp.float32)
    blocks = down_matrix.reshape(N_TP, FF // N_TP, D).astype(jnp.float32)
    parts = jnp.einsum("rgf,gfd->rgd", groups, blocks, precision=lax.Precision.HIGHEST).astype(jnp.bfloat16)
    return jnp.sum(parts.astype(jnp.float32), axis=1).astype(jnp.bfloat16)


def one_batch(batch_tokens, batch_routes, batch_gain, w_gate, w_up, w_down):
    pair_count = TOKENS * TOP
    flat_ids = batch_routes.reshape(pair_count).astype(jnp.int32)
    expert_indicator = (flat_ids[:, None] == jnp.arange(E, dtype=jnp.int32)[None, :]).astype(jnp.int32)
    running = (jnp.cumsum(expert_indicator, axis=0) - 1).astype(jnp.int32)
    slot_rank = jnp.sum(running * expert_indicator, axis=1).astype(jnp.int32)
    slot_table = jnp.full((E, N_EP * CAP), pair_count, dtype=jnp.int32)
    slot_table = slot_table.at[flat_ids, slot_rank].set(jnp.arange(pair_count, dtype=jnp.int32))
    padded = jnp.concatenate([batch_tokens, jnp.zeros((1, D), batch_tokens.dtype)], axis=0)

    def visit(collected, expert):
        pair_ids = slot_table[expert]
        row_block = padded[pair_ids // TOP]
        expert_out = expert_rows(row_block, w_gate[expert], w_up[expert], w_down[expert])
        return collected.at[pair_ids].set(expert_out.astype(jnp.float32)), None

    collected = jnp.zeros((pair_count + 1, D), jnp.float32)
    collected, _ = lax.scan(visit, collected, jnp.arange(E, dtype=jnp.int32))
    outputs = collected[:pair_count].reshape(TOKENS, TOP, D)
    return jnp.sum(batch_gain[:, :, None] * outputs, axis=1).astype(jnp.bfloat16)


def reference(tokens, routes, route_weight, w_gate, w_up, w_down):
    results = []
    for batch_index in range(MB):
        results.append(one_batch(tokens[batch_index], routes[batch_index], route_weight[batch_index], w_gate, w_up, w_down))
    return jnp.stack(results, axis=0)
```

```python
import functools

import jax
import jax.numpy as jnp
from jax import lax
from jax.experimental import pallas as pl
from jax.experimental.pallas import tpu as pltpu
from jax.sharding import PartitionSpec as P

MESH = pl.DeviceIdType.MESH
CHUNKS = 4
OFFSETS = (0, 0, 3, 3)


def log2(n):
    return n.bit_length() - 1


def kernel(
    n_ep, n_tp, batches, cap,
    routes_t, gains_t, tokens, w_gate, w_up, w_down, out,
    outgoing, gathered, combine, w_in, w_out, total, hidden,
    sum_right, sum_left, got_right, got_left, answer, returned,
    own_sem, w_sem, go_send, go_recv, ag_send, ag_recv,
    right_send, right_recv, left_send, left_recv, back_send, back_recv,
):
    me = lax.axis_index("ep")
    place = lax.axis_index("tp")
    right, left = lax.rem(place + 1, n_tp), lax.rem(place + n_tp - 1, n_tp)
    per = n_ep // CHUNKS
    group, seat = lax.div(me, per), lax.rem(me, per)
    top, toks = routes_t.shape
    rows = batches * cap
    slots = n_ep * rows
    features = tokens.shape[1]
    units = w_gate.shape[2]
    many = per * rows

    def reach(c):
        far = n_tp // 2
        near = n_tp - 1 - far
        return (far, near) if c % 2 == 0 else (near, far)

    weight_copies = [
        pltpu.make_async_copy(w_gate, w_in.at[:, :, pl.ds(0, units)], w_sem.at[0]),
        pltpu.make_async_copy(w_up, w_in.at[:, :, pl.ds(units, units)], w_sem.at[1]),
    ] + [
        pltpu.make_async_copy(
            w_down.at[:, pl.ds(g * features, features)], w_out.at[g], w_sem.at[2 + g]
        )
        for g in range(n_tp)
    ]
    for copy in weight_copies:
        copy.start()

    barrier = pltpu.get_barrier_semaphore()

    @pl.loop(1, n_ep)
    def _(i):
        pl.semaphore_signal(
            barrier, inc=1, device_id={"ep": lax.rem(me + i, n_ep)}, device_id_type=MESH
        )

    neighbours = (left, right) if n_tp > 2 else (right,)
    for neighbour in neighbours:
        pl.semaphore_signal(barrier, inc=1, device_id={"tp": neighbour}, device_id_type=MESH)

    slot = lax.broadcasted_iota(jnp.int32, (slots, toks), 0)
    token = lax.broadcasted_iota(jnp.int32, (slots, toks), 1)
    expert = slot >> log2(rows)
    hits = jnp.zeros((slots, toks), jnp.float32)
    gains = jnp.zeros((slots, toks), jnp.float32)
    for k in range(top):
        match = routes_t[k : k + 1, :] == expert
        hits += jnp.where(match, 1.0, 0.0)
        gains += jnp.where(match, gains_t[k : k + 1, :], 0.0)
    block = log2(toks // batches)
    first = lax.broadcasted_iota(jnp.int32, (toks, toks), 0)
    second = lax.broadcasted_iota(jnp.int32, (toks, toks), 1)
    earlier = jnp.where(
        (first < second) & ((first >> block) == (second >> block)), 1.0, 0.0
    ).astype(jnp.bfloat16)
    rank = jnp.dot(hits.astype(jnp.bfloat16), earlier, preferred_element_type=jnp.float32)
    wanted = (slot & (cap - 1)).astype(jnp.float32)
    same = ((slot & (rows - 1)) >> log2(cap)) == (token >> block)
    picked = jnp.where((rank == wanted) & same, hits, 0.0)
    combine[...] = picked * gains
    outgoing[...] = (
        jnp.dot(picked.astype(jnp.bfloat16), tokens[...], preferred_element_type=jnp.float32)
        .reshape(n_ep, rows, features)
        .astype(jnp.bfloat16)
    )

    pl.semaphore_wait(barrier, n_ep - 1 + len(neighbours))

    own_go = pltpu.make_async_copy(outgoing.at[me], gathered.at[0, 0, seat], own_sem.at[0])
    own_go.start()
    for c in range(CHUNKS):

        @pl.loop(1 if c == 0 else 0, per)
        def _(i):
            peer = lax.rem(group + c, CHUNKS) * per + lax.rem(seat + i, per)
            pltpu.make_async_remote_copy(
                src_ref=outgoing.at[peer],
                dst_ref=gathered.at[c, 0, seat],
                send_sem=go_send.at[c],
                recv_sem=go_recv.at[c],
                device_id={"ep": peer},
                device_id_type=MESH,
            ).start()

    def go_bytes(c):
        n = per - 1 if c == 0 else per
        if n == 0:
            return None
        return pltpu.make_async_remote_copy(
            src_ref=outgoing.at[pl.ds(0, n)],
            dst_ref=gathered.at[c, 0, pl.ds(0, n)],
            send_sem=go_send.at[c],
            recv_sem=go_recv.at[c],
            device_id={"tp": right},
            device_id_type=MESH,
        )

    def back_bytes(c):
        n = per - 1 if c == 0 else per
        if n == 0:
            return None
        return pltpu.make_async_remote_copy(
            src_ref=answer.at[c, pl.ds(0, n)],
            dst_ref=returned.at[pl.ds(0, n)],
            send_sem=back_send.at[c],
            recv_sem=back_recv.at[c],
            device_id={"tp": right},
            device_id_type=MESH,
        )

    def pass_on(c, source, slot_id, neighbour):
        return pltpu.make_async_remote_copy(
            src_ref=gathered.at[c, source],
            dst_ref=gathered.at[c, slot_id],
            send_sem=ag_send.at[c, slot_id],
            recv_sem=ag_recv.at[c, slot_id],
            device_id={"tp": neighbour},
            device_id_type=MESH,
        )

    def multiply(c, slot_id, origin):
        value = gathered[c, slot_id].astype(jnp.float32).reshape(many, features)
        return jnp.dot(
            value.astype(jnp.bfloat16), w_in[origin], preferred_element_type=jnp.float32
        )

    gather_copies, ring_copies = [], []

    def gather_begin(c):
        to_right, to_left = reach(c)
        if c == 0:
            own_go.wait()
        arrived = go_bytes(c)
        if arrived is not None:
            arrived.wait_recv()
        for length, slot_id, neighbour in ((to_right, 1, right), (to_left, to_right + 1, left)):
            if length > 0:
                copy = pass_on(c, 0, slot_id, neighbour)
                copy.start()
                gather_copies.append(copy)
        if c == 0:
            weight_copies[0].wait()
            weight_copies[1].wait()
        total[c] = multiply(c, 0, place)

    def gather_hop(c, j):
        to_right, to_left = reach(c)
        todo = []
        for length, base, neighbour, step in (
            (to_right, 0, right, n_tp - j),
            (to_left, to_right, left, j),
        ):
            if j <= length:
                pass_on(c, 0, base + j, neighbour).wait_recv()
                if j < length:
                    copy = pass_on(c, base + j, base + j + 1, neighbour)
                    copy.start()
                    gather_copies.append(copy)
                todo.append((base + j, lax.rem(place + step, n_tp)))
        for slot_id, origin in todo:
            total[c] += multiply(c, slot_id, origin)

    def activate(c):
        gate, up = total[c, :, :units], total[c, :, units:]
        hidden[c] = (gate / (1.0 + jnp.exp(-gate)) * up).astype(jnp.bfloat16)

    def part(c, target):
        return jnp.dot(hidden[c], w_out[target], preferred_element_type=jnp.float32)

    def ring(c, j, to_right):
        sums, got, send, recv, neighbour = (
            (sum_right, got_right, right_send, right_recv, right)
            if to_right
            else (sum_left, got_left, left_send, left_recv, left)
        )
        return pltpu.make_async_remote_copy(
            src_ref=sums.at[c, j],
            dst_ref=got.at[c, j],
            send_sem=send.at[c, j],
            recv_sem=recv.at[c, j],
            device_id={"tp": neighbour},
            device_id_type=MESH,
        )

    def reduce_step(c, j):
        if j == 0:
            if c == 0:
                for copy in weight_copies[2:]:
                    copy.wait()
            activate(c)
        for length, to_right in zip(reach(c), (True, False)):
            if j < length:
                ahead = length - j if to_right else n_tp - (length - j)
                value = part(c, lax.rem(place + ahead, n_tp))
                sums, got = (sum_right, got_right) if to_right else (sum_left, got_left)
                if j > 0:
                    ring(c, j - 1, to_right).wait_recv()
                    value += got[c, j - 1].astype(jnp.float32)
                sums[c, j] = value.astype(jnp.bfloat16)
                copy = ring(c, j, to_right)
                copy.start()
                ring_copies.append(copy)

    own_back = pltpu.make_async_copy(answer.at[0, seat], returned.at[me], own_sem.at[1])

    def reduce_end(c):
        value = part(c, place)
        for length, to_right in zip(reach(c), (True, False)):
            if length > 0:
                ring(c, length - 1, to_right).wait_recv()
                got = got_right if to_right else got_left
                value += got[c, length - 1].astype(jnp.float32)
        answer[c] = value.reshape(per, rows, features).astype(jnp.bfloat16)
        if c == 0:
            own_back.start()

        @pl.loop(1 if c == 0 else 0, per)
        def _(i):
            other = lax.rem(seat + i, per)
            peer = lax.rem(group + CHUNKS - c, CHUNKS) * per + other
            pltpu.make_async_remote_copy(
                src_ref=answer.at[c, other],
                dst_ref=returned.at[me],
                send_sem=back_send.at[c],
                recv_sem=back_recv.at[c],
                device_id={"ep": peer},
                device_id_type=MESH,
            ).start()

    hops = n_tp // 2
    events = []
    for c in range(CHUNKS):
        start = OFFSETS[c]
        events.append((start, c, functools.partial(gather_begin, c)))
        for j in range(1, hops + 1):
            events.append((start + j, c, functools.partial(gather_hop, c, j)))
        for j in range(hops):
            events.append((start + hops + 1 + j, c, functools.partial(reduce_step, c, j)))
        events.append((start + 2 * hops + 1, c, functools.partial(reduce_end, c)))
    for _, _, run in sorted(events, key=lambda event: event[:2]):
        run()

    own_back.wait()
    for c in range(CHUNKS):
        arrived = back_bytes(c)
        if arrived is not None:
            arrived.wait_recv()
    values = returned[...].astype(jnp.float32).reshape(slots, features).astype(jnp.bfloat16)
    weights = combine[...]
    high = weights.astype(jnp.bfloat16)
    low = (weights - high.astype(jnp.float32)).astype(jnp.bfloat16)
    over_slots = (((0,), (0,)), ((), ()))
    mixed = lax.dot_general(high, values, over_slots, preferred_element_type=jnp.float32)
    mixed += lax.dot_general(low, values, over_slots, preferred_element_type=jnp.float32)
    out[...] = mixed.astype(jnp.bfloat16)

    for c in range(CHUNKS):
        for sent in (go_bytes(c), back_bytes(c)):
            if sent is not None:
                sent.wait_send()
    for copy in gather_copies + ring_copies:
        copy.wait_send()


def shards(tokens, routes, route_weight, w_gate, w_up, w_down):
    n_ep, n_tp = lax.axis_size("ep"), lax.axis_size("tp")
    batches, tok_rows, features = tokens.shape
    top = routes.shape[2]
    cap = 2 * tok_rows * top // n_ep
    toks, rows = batches * tok_rows, batches * cap
    units = w_gate.shape[2]
    per = n_ep // CHUNKS
    many = per * rows
    hops = n_tp // 2
    dma = pltpu.SemaphoreType.DMA
    vmem = pl.BlockSpec(memory_space=pltpu.VMEM)
    hbm = pl.BlockSpec(memory_space=pl.ANY)
    bf16, f32 = jnp.bfloat16, jnp.float32
    ring = pltpu.VMEM((CHUNKS, hops, many, features), bf16)
    out = pl.pallas_call(
        functools.partial(kernel, n_ep, n_tp, batches, cap),
        out_shape=jax.ShapeDtypeStruct((toks, features), bf16),
        in_specs=[vmem, vmem, vmem, hbm, hbm, hbm],
        out_specs=vmem,
        scratch_shapes=[
            pltpu.VMEM((n_ep, rows, features), bf16),
            pltpu.VMEM((CHUNKS, n_tp, per, rows, features), bf16),
            pltpu.VMEM((n_ep * rows, toks), f32),
            pltpu.VMEM((n_tp, features, 2 * units), bf16),
            pltpu.VMEM((n_tp, units, features), bf16),
            pltpu.VMEM((CHUNKS, many, 2 * units), f32),
            pltpu.VMEM((CHUNKS, many, units), bf16),
            ring,
            ring,
            ring,
            ring,
            pltpu.VMEM((CHUNKS, per, rows, features), bf16),
            pltpu.VMEM((n_ep, rows, features), bf16),
            dma((2,)),
            dma((2 + n_tp,)),
            dma((CHUNKS,)),
            dma((CHUNKS,)),
            dma((CHUNKS, n_tp)),
            dma((CHUNKS, n_tp)),
            dma((CHUNKS, hops)),
            dma((CHUNKS, hops)),
            dma((CHUNKS, hops)),
            dma((CHUNKS, hops)),
            dma((CHUNKS,)),
            dma((CHUNKS,)),
        ],
        compiler_params=pltpu.CompilerParams(
            collective_id=0, has_side_effects=True, vmem_limit_bytes=48 * 1024 * 1024
        ),
        name="expert_layer",
    )(
        routes.reshape(toks, top).T,
        route_weight.reshape(toks, top).T,
        tokens.reshape(toks, features),
        w_gate.reshape(n_tp, features, units),
        w_up.reshape(n_tp, features, units),
        w_down.reshape(units, n_tp * features),
    )
    return out.reshape(batches, tok_rows, features)


def solution(mesh):
    return jax.shard_map(
        shards,
        mesh=mesh,
        in_specs=(
            P(None, "ep", "tp"),
            P(None, "ep", None),
            P(None, "ep", None),
            P("ep", None, "tp"),
            P("ep", None, "tp"),
            P("ep", "tp", None),
        ),
        out_specs=P(None, "ep", "tp"),
        check_vma=False,
    )
```

```python
import functools

import jax
import jax.numpy as jnp
from jax import lax
from jax.experimental import pallas as pl
from jax.experimental.pallas import tpu as pltpu
from jax.sharding import PartitionSpec as P

MESH = pl.DeviceIdType.MESH
CHUNKS = 4
OFFSETS = (0, 1, 2, 3)
FAR_AT = 0.5


def log2(n):
    return n.bit_length() - 1


def kernel(
    n_ep, n_tp, batches, cap,
    routes_in, gains_in, tokens_in, w_gate, w_up, w_down, out,
    routes, weights, tokens, outgoing, gathered, combine, w_in, w_out, total, hidden,
    sum_right, sum_left, got_right, got_left, answer, returned,
    far_tokens, far_outgoing, far_answer, far_returned, far_mixed, far_got,
    in_sem, own_sem, w_sem, go_send, go_recv, ag_send, ag_recv,
    right_send, right_recv, left_send, left_recv, back_send, back_recv,
    far_send, far_recv, far_go_send, far_go_recv, far_back_send, far_back_recv,
):
    me = lax.axis_index("ep")
    place = lax.axis_index("tp")
    right, left = lax.rem(place + 1, n_tp), lax.rem(place + n_tp - 1, n_tp)
    opposite = lax.rem(place + n_tp // 2, n_tp)
    hops = n_tp // 2 - 1
    per = n_ep // CHUNKS
    group, seat = lax.div(me, per), lax.rem(me, per)
    top, toks = routes.shape[1], tokens.shape[0]
    rows = batches * cap
    slots = n_ep * rows
    features = tokens.shape[1]
    units = w_gate.shape[2]
    many = per * rows

    small_copies = [
        pltpu.make_async_copy(source, target, in_sem.at[i])
        for i, (source, target) in enumerate(
            ((routes_in, routes), (gains_in, weights), (tokens_in, tokens))
        )
    ]
    for copy in small_copies:
        copy.start()

    weight_copies = [
        pltpu.make_async_copy(w_gate, w_in.at[:, :, pl.ds(0, units)], w_sem.at[0]),
        pltpu.make_async_copy(w_up, w_in.at[:, :, pl.ds(units, units)], w_sem.at[1]),
    ] + [
        pltpu.make_async_copy(
            w_down.at[:, pl.ds(g * features, features)], w_out.at[g], w_sem.at[2 + g]
        )
        for g in range(n_tp)
    ]
    for copy in weight_copies:
        copy.start()

    barrier = pltpu.get_barrier_semaphore()

    @pl.loop(1, n_ep)
    def _(i):
        pl.semaphore_signal(
            barrier, inc=1, device_id={"ep": lax.rem(me + i, n_ep)}, device_id_type=MESH
        )

    neighbours = (left, right, opposite)
    for neighbour in neighbours:
        pl.semaphore_signal(barrier, inc=1, device_id={"tp": neighbour}, device_id_type=MESH)

    for copy in small_copies:
        copy.wait()
    token = lax.broadcasted_iota(jnp.int32, (toks, slots), 0)
    slot = lax.broadcasted_iota(jnp.int32, (toks, slots), 1)
    expert = slot >> log2(rows)
    hits = jnp.zeros((toks, slots), jnp.float32)
    gains = jnp.zeros((toks, slots), jnp.float32)
    chosen = jnp.concatenate([routes[b].T for b in range(batches)], axis=0)
    factor = jnp.concatenate([weights[b].T for b in range(batches)], axis=0)
    for k in range(top):
        match = chosen[:, k : k + 1] == expert
        hits += jnp.where(match, 1.0, 0.0)
        gains += jnp.where(match, factor[:, k : k + 1], 0.0)
    block = log2(toks // batches)
    first = lax.broadcasted_iota(jnp.int32, (toks, toks), 0)
    second = lax.broadcasted_iota(jnp.int32, (toks, toks), 1)
    earlier = jnp.where(
        (second < first) & ((first >> block) == (second >> block)), 1.0, 0.0
    ).astype(jnp.bfloat16)
    rank = jnp.dot(earlier, hits.astype(jnp.bfloat16), preferred_element_type=jnp.float32)
    wanted = (slot & (cap - 1)).astype(jnp.float32)
    same = ((slot & (rows - 1)) >> log2(cap)) == (token >> block)
    picked = jnp.where((rank == wanted) & same, hits, 0.0)
    combine[...] = picked * gains
    def place_tokens(source, target):
        rows_out = lax.dot_general(
            picked.astype(jnp.bfloat16),
            source[...],
            (((0,), (0,)), ((), ())),
            preferred_element_type=jnp.float32,
        )
        target[...] = rows_out.reshape(n_ep, rows, features).astype(jnp.bfloat16)

    place_tokens(tokens, outgoing)

    pl.semaphore_wait(barrier, n_ep - 1 + len(neighbours))

    def far_copy(source, target, i):
        return pltpu.make_async_remote_copy(
            src_ref=source,
            dst_ref=target,
            send_sem=far_send.at[i],
            recv_sem=far_recv.at[i],
            device_id={"tp": opposite},
            device_id_type=MESH,
        )

    token_swap = far_copy(tokens, far_tokens, 0)
    token_swap.start()

    def go(source, slot_id, own, send, recv):
        own.start()
        for c in range(CHUNKS):

            @pl.loop(1 if c == 0 else 0, per)
            def _(i):
                peer = lax.rem(group + c, CHUNKS) * per + lax.rem(seat + i, per)
                pltpu.make_async_remote_copy(
                    src_ref=source.at[peer],
                    dst_ref=gathered.at[c, slot_id, seat],
                    send_sem=send.at[c],
                    recv_sem=recv.at[c],
                    device_id={"ep": peer},
                    device_id_type=MESH,
                ).start()

    own_go = pltpu.make_async_copy(outgoing.at[me], gathered.at[0, 0, seat], own_sem.at[0])
    go(outgoing, 0, own_go, go_send, go_recv)
    far_slot = n_tp - 1
    own_far_go = pltpu.make_async_copy(
        far_outgoing.at[me], gathered.at[0, far_slot, seat], own_sem.at[2]
    )

    def far_dispatch():
        token_swap.wait_recv()
        place_tokens(far_tokens, far_outgoing)
        go(far_outgoing, far_slot, own_far_go, far_go_send, far_go_recv)

    def all_bytes(c, source, target, send, recv):
        n = per - 1 if c == 0 else per
        if n == 0:
            return None
        return pltpu.make_async_remote_copy(
            src_ref=source.at[pl.ds(0, n)],
            dst_ref=target.at[pl.ds(0, n)],
            send_sem=send.at[c],
            recv_sem=recv.at[c],
            device_id={"tp": right},
            device_id_type=MESH,
        )

    def go_bytes(c):
        return all_bytes(c, outgoing, gathered.at[c, 0], go_send, go_recv)

    def far_go_bytes(c):
        return all_bytes(c, far_outgoing, gathered.at[c, far_slot], far_go_send, far_go_recv)

    def back_bytes(c):
        return all_bytes(c, answer.at[c], returned, back_send, back_recv)

    def far_back_bytes(c):
        return all_bytes(c, far_answer.at[c], far_returned, far_back_send, far_back_recv)

    def pass_on(c, source, slot_id, neighbour):
        return pltpu.make_async_remote_copy(
            src_ref=gathered.at[c, source],
            dst_ref=gathered.at[c, slot_id],
            send_sem=ag_send.at[c, slot_id],
            recv_sem=ag_recv.at[c, slot_id],
            device_id={"tp": neighbour},
            device_id_type=MESH,
        )

    def multiply(c, slot_id, origin):
        value = gathered[c, slot_id].astype(jnp.float32).reshape(many, features)
        return jnp.dot(
            value.astype(jnp.bfloat16), w_in[origin], preferred_element_type=jnp.float32
        )

    gather_copies, ring_copies = [], []

    def gather_begin(c):
        to_right, to_left = hops, hops
        if c == 0:
            own_go.wait()
        arrived = go_bytes(c)
        if arrived is not None:
            arrived.wait_recv()
        for length, slot_id, neighbour in ((to_right, 1, right), (to_left, to_right + 1, left)):
            if length > 0:
                copy = pass_on(c, 0, slot_id, neighbour)
                copy.start()
                gather_copies.append(copy)
        if c == 0:
            weight_copies[0].wait()
            weight_copies[1].wait()
        total[c] = multiply(c, 0, place)

    def gather_hop(c, j):
        to_right, to_left = hops, hops
        todo = []
        for length, base, neighbour, step in (
            (to_right, 0, right, n_tp - j),
            (to_left, to_right, left, j),
        ):
            if j <= length:
                pass_on(c, 0, base + j, neighbour).wait_recv()
                if j < length:
                    copy = pass_on(c, base + j, base + j + 1, neighbour)
                    copy.start()
                    gather_copies.append(copy)
                todo.append((base + j, lax.rem(place + step, n_tp)))
        for slot_id, origin in todo:
            total[c] += multiply(c, slot_id, origin)

    def far_gather(c):
        if c == 0:
            own_far_go.wait()
        arrived = far_go_bytes(c)
        if arrived is not None:
            arrived.wait_recv()
        total[c] += multiply(c, far_slot, opposite)

    def activate(c):
        gate, up = total[c, :, :units], total[c, :, units:]
        hidden[c] = (gate / (1.0 + jnp.exp(-gate)) * up).astype(jnp.bfloat16)

    def part(c, target):
        return jnp.dot(hidden[c], w_out[target], preferred_element_type=jnp.float32)

    def ring(c, j, to_right):
        sums, got, send, recv, neighbour = (
            (sum_right, got_right, right_send, right_recv, right)
            if to_right
            else (sum_left, got_left, left_send, left_recv, left)
        )
        return pltpu.make_async_remote_copy(
            src_ref=sums.at[c, j],
            dst_ref=got.at[c, j],
            send_sem=send.at[c, j],
            recv_sem=recv.at[c, j],
            device_id={"tp": neighbour},
            device_id_type=MESH,
        )

    def reduce_step(c, j):
        if j == 0:
            if c == 0:
                for copy in weight_copies[2:]:
                    copy.wait()
            activate(c)
        for length, to_right in ((hops, True), (hops, False)):
            if j < length:
                ahead = length - j if to_right else n_tp - (length - j)
                value = part(c, lax.rem(place + ahead, n_tp))
                sums, got = (sum_right, got_right) if to_right else (sum_left, got_left)
                if j > 0:
                    ring(c, j - 1, to_right).wait_recv()
                    value += got[c, j - 1].astype(jnp.float32)
                sums[c, j] = value.astype(jnp.bfloat16)
                copy = ring(c, j, to_right)
                copy.start()
                ring_copies.append(copy)

    def back(c, source, target, own, send, recv):
        if c == 0:
            own.start()

        @pl.loop(1 if c == 0 else 0, per)
        def _(i):
            other = lax.rem(seat + i, per)
            peer = lax.rem(group + CHUNKS - c, CHUNKS) * per + other
            pltpu.make_async_remote_copy(
                src_ref=source.at[c, other],
                dst_ref=target.at[me],
                send_sem=send.at[c],
                recv_sem=recv.at[c],
                device_id={"ep": peer},
                device_id_type=MESH,
            ).start()

    own_back = pltpu.make_async_copy(answer.at[0, seat], returned.at[me], own_sem.at[1])
    own_far_back = pltpu.make_async_copy(
        far_answer.at[0, seat], far_returned.at[me], own_sem.at[3]
    )

    def far_reduce(c):
        value = part(c, opposite)
        far_answer[c] = value.reshape(per, rows, features).astype(jnp.bfloat16)
        back(c, far_answer, far_returned, own_far_back, far_back_send, far_back_recv)

    def reduce_end(c):
        value = part(c, place)
        for length, to_right in ((hops, True), (hops, False)):
            if length > 0:
                ring(c, length - 1, to_right).wait_recv()
                got = got_right if to_right else got_left
                value += got[c, length - 1].astype(jnp.float32)
        answer[c] = value.reshape(per, rows, features).astype(jnp.bfloat16)
        back(c, answer, returned, own_back, back_send, back_recv)

    events = [(FAR_AT, -1, far_dispatch)]
    for c in range(CHUNKS):
        start = OFFSETS[c]
        events.append((start, c, functools.partial(gather_begin, c)))
        for j in range(1, hops + 1):
            events.append((start + j, c, functools.partial(gather_hop, c, j)))
        events.append((start + hops, c, functools.partial(far_gather, c)))
        start += hops + 1
        for j in range(hops):
            events.append((start + j, c, functools.partial(reduce_step, c, j)))
        events.append((start, c, functools.partial(far_reduce, c)))
        events.append((start + hops, c, functools.partial(reduce_end, c)))
    for _, _, run in sorted(events, key=lambda event: event[:2]):
        run()

    scale = combine[...]
    high = scale.astype(jnp.bfloat16)
    low = (scale - high.astype(jnp.float32)).astype(jnp.bfloat16)

    def mix(source, own, arrivals):
        own.wait()
        for c in range(CHUNKS):
            arrived = arrivals(c)
            if arrived is not None:
                arrived.wait_recv()
        values = source[...].astype(jnp.float32).reshape(slots, features).astype(jnp.bfloat16)
        mixed = jnp.dot(high, values, preferred_element_type=jnp.float32)
        return mixed + jnp.dot(low, values, preferred_element_type=jnp.float32)

    far_mixed[...] = mix(far_returned, own_far_back, far_back_bytes)
    mixed_swap = far_copy(far_mixed, far_got, 1)
    mixed_swap.start()
    mixed = mix(returned, own_back, back_bytes)
    mixed_swap.wait_recv()
    out[...] = (mixed + far_got[...]).astype(jnp.bfloat16)

    for c in range(CHUNKS):
        for sent in (go_bytes(c), far_go_bytes(c), back_bytes(c), far_back_bytes(c)):
            if sent is not None:
                sent.wait_send()
    for copy in gather_copies + ring_copies + [token_swap, mixed_swap]:
        copy.wait_send()


def shards(tokens, routes, route_weight, w_gate, w_up, w_down):
    n_ep, n_tp = lax.axis_size("ep"), lax.axis_size("tp")
    batches, tok_rows, features = tokens.shape
    top = routes.shape[2]
    cap = 2 * tok_rows * top // n_ep
    toks, rows = batches * tok_rows, batches * cap
    units = w_gate.shape[2]
    per = n_ep // CHUNKS
    many = per * rows
    hops = n_tp // 2 - 1
    dma = pltpu.SemaphoreType.DMA
    vmem = pl.BlockSpec(memory_space=pltpu.VMEM)
    hbm = pl.BlockSpec(memory_space=pltpu.HBM)
    bf16, f32 = jnp.bfloat16, jnp.float32
    ring = pltpu.VMEM((CHUNKS, hops, many, features), bf16)
    out = pl.pallas_call(
        functools.partial(kernel, n_ep, n_tp, batches, cap),
        out_shape=jax.ShapeDtypeStruct((toks, features), bf16),
        in_specs=[hbm] * 6,
        out_specs=vmem,
        scratch_shapes=[
            pltpu.VMEM((batches, top, tok_rows), jnp.int32),
            pltpu.VMEM((batches, top, tok_rows), f32),
            pltpu.VMEM((toks, features), bf16),
            pltpu.VMEM((n_ep, rows, features), bf16),
            pltpu.VMEM((CHUNKS, n_tp, per, rows, features), bf16),
            pltpu.VMEM((toks, n_ep * rows), f32),
            pltpu.VMEM((n_tp, features, 2 * units), bf16),
            pltpu.VMEM((n_tp, units, features), bf16),
            pltpu.VMEM((CHUNKS, many, 2 * units), f32),
            pltpu.VMEM((CHUNKS, many, units), bf16),
            ring,
            ring,
            ring,
            ring,
            pltpu.VMEM((CHUNKS, per, rows, features), bf16),
            pltpu.VMEM((n_ep, rows, features), bf16),
            pltpu.VMEM((toks, features), bf16),
            pltpu.VMEM((n_ep, rows, features), bf16),
            pltpu.VMEM((CHUNKS, per, rows, features), bf16),
            pltpu.VMEM((n_ep, rows, features), bf16),
            pltpu.VMEM((toks, features), f32),
            pltpu.VMEM((toks, features), f32),
            dma((3,)),
            dma((4,)),
            dma((2 + n_tp,)),
            dma((CHUNKS,)),
            dma((CHUNKS,)),
            dma((CHUNKS, n_tp)),
            dma((CHUNKS, n_tp)),
            dma((CHUNKS, hops)),
            dma((CHUNKS, hops)),
            dma((CHUNKS, hops)),
            dma((CHUNKS, hops)),
            dma((CHUNKS,)),
            dma((CHUNKS,)),
            dma((2,)),
            dma((2,)),
            dma((CHUNKS,)),
            dma((CHUNKS,)),
            dma((CHUNKS,)),
            dma((CHUNKS,)),
        ],
        compiler_params=pltpu.CompilerParams(
            collective_id=0, has_side_effects=True, vmem_limit_bytes=67_043_328
        ),
        name="expert_layer",
    )(
        routes.swapaxes(1, 2),
        route_weight.swapaxes(1, 2),
        tokens.reshape(toks, features),
        w_gate.reshape(n_tp, features, units),
        w_up.reshape(n_tp, features, units),
        w_down.reshape(units, n_tp * features),
    )
    return out.reshape(batches, tok_rows, features)


def solution(mesh):
    return jax.shard_map(
        shards,
        mesh=mesh,
        in_specs=(
            P(None, "ep", "tp"),
            P(None, "ep", None),
            P(None, "ep", None),
            P("ep", None, "tp"),
            P("ep", None, "tp"),
            P("ep", "tp", None),
        ),
        out_specs=P(None, "ep", "tp"),
        check_vma=False,
    )
```

```python
import functools

import jax
import jax.numpy as jnp
from jax import lax
from jax.experimental import pallas as pl
from jax.experimental.pallas import tpu as pltpu
from jax.sharding import PartitionSpec as P

MESH = pl.DeviceIdType.MESH
DISTANCES = ((0,), (1,), (4,), (-3,), (3,), (-2,), (2,), (-1,))
DEPTH = 8
CORES = 2
CHUNKS = len(DISTANCES)
OFFSETS = (0, 0.5, 1, 1.5, 2, 2.5, 3, 3.5)
FAR_AT = 0.75


def log2(n):
    return n.bit_length() - 1


def kernel(
    n_ep, n_tp, batches, cap,
    routes_in, gains_in, tokens_in, w_gate, w_up, w_down, out,
    routes, weights, tokens, outgoing, gathered, combine, w_in, w_out, total, hidden,
    sum_right, sum_left, got_right, got_left, answer, returned,
    far_tokens, far_outgoing, far_answer, far_returned, far_mixed, far_got,
    in_sem, own_sem, w_sem, go_send, go_recv, ag_send, ag_recv,
    right_send, right_recv, left_send, left_recv, back_send, back_recv,
    far_send, far_recv, far_go_send, far_go_recv, far_back_send, far_back_recv,
):
    me = lax.axis_index("ep")
    place = lax.axis_index("tp")
    right, left = lax.rem(place + 1, n_tp), lax.rem(place + n_tp - 1, n_tp)
    opposite = lax.rem(place + n_tp // 2, n_tp)
    hops = n_tp // 2 - 1
    per = n_ep // CHUNKS
    core, z = lax.rem(me, CORES), lax.rem(lax.div(me, CORES), DEPTH)
    x = lax.div(me, CORES * DEPTH)
    layers = n_ep // DEPTH
    layer = x * CORES + core
    width = DEPTH // CHUNKS
    seat = layer * width

    def mate(c, i, sign):
        steps = DISTANCES[c]
        other = lax.rem(layer + lax.div(i, width), layers)
        q = lax.rem(i, width)
        far = steps[0] + q * (steps[-1] - steps[0])
        deep = lax.rem(z + sign * far + DEPTH, DEPTH)
        peer = (lax.div(other, CORES) * DEPTH + deep) * CORES + lax.rem(other, CORES)
        return peer, seat + q, other * width + q

    top, toks = routes.shape[1], tokens.shape[0]
    rows = batches * cap
    slots = n_ep * rows
    features = tokens.shape[1]
    units = w_gate.shape[2]
    many = per * rows

    small_copies = [
        pltpu.make_async_copy(source, target, in_sem.at[i])
        for i, (source, target) in enumerate(
            ((routes_in, routes), (gains_in, weights), (tokens_in, tokens))
        )
    ]
    for copy in small_copies:
        copy.start()

    weight_copies = [
        pltpu.make_async_copy(w_gate, w_in.at[:, :, pl.ds(0, units)], w_sem.at[0]),
        pltpu.make_async_copy(w_up, w_in.at[:, :, pl.ds(units, units)], w_sem.at[1]),
    ] + [
        pltpu.make_async_copy(
            w_down.at[:, pl.ds(g * features, features)], w_out.at[g], w_sem.at[2 + g]
        )
        for g in range(n_tp)
    ]
    for copy in weight_copies:
        copy.start()

    barrier = pltpu.get_barrier_semaphore()

    @pl.loop(1, n_ep)
    def _(i):
        pl.semaphore_signal(
            barrier, inc=1, device_id={"ep": lax.rem(me + i, n_ep)}, device_id_type=MESH
        )

    neighbours = (left, right, opposite)
    for neighbour in neighbours:
        pl.semaphore_signal(barrier, inc=1, device_id={"tp": neighbour}, device_id_type=MESH)

    for copy in small_copies:
        copy.wait()
    token = lax.broadcasted_iota(jnp.int32, (toks, slots), 0)
    slot = lax.broadcasted_iota(jnp.int32, (toks, slots), 1)
    expert = slot >> log2(rows)
    hits = jnp.zeros((toks, slots), jnp.float32)
    gains = jnp.zeros((toks, slots), jnp.float32)
    chosen = jnp.concatenate([routes[b].T for b in range(batches)], axis=0)
    factor = jnp.concatenate([weights[b].T for b in range(batches)], axis=0)
    for k in range(top):
        match = chosen[:, k : k + 1] == expert
        hits += jnp.where(match, 1.0, 0.0)
        gains += jnp.where(match, factor[:, k : k + 1], 0.0)
    block = log2(toks // batches)
    first = lax.broadcasted_iota(jnp.int32, (toks, toks), 0)
    second = lax.broadcasted_iota(jnp.int32, (toks, toks), 1)
    earlier = jnp.where(
        (second < first) & ((first >> block) == (second >> block)), 1.0, 0.0
    ).astype(jnp.bfloat16)
    rank = jnp.dot(earlier, hits.astype(jnp.bfloat16), preferred_element_type=jnp.float32)
    wanted = (slot & (cap - 1)).astype(jnp.float32)
    same = ((slot & (rows - 1)) >> log2(cap)) == (token >> block)
    picked = jnp.where((rank == wanted) & same, hits, 0.0)
    combine[...] = picked * gains
    def place_tokens(source, target):
        rows_out = lax.dot_general(
            picked.astype(jnp.bfloat16),
            source[...],
            (((0,), (0,)), ((), ())),
            preferred_element_type=jnp.float32,
        )
        target[...] = rows_out.reshape(n_ep, rows, features).astype(jnp.bfloat16)

    place_tokens(tokens, outgoing)

    pl.semaphore_wait(barrier, n_ep - 1 + len(neighbours))

    def far_copy(source, target, i):
        return pltpu.make_async_remote_copy(
            src_ref=source,
            dst_ref=target,
            send_sem=far_send.at[i],
            recv_sem=far_recv.at[i],
            device_id={"tp": opposite},
            device_id_type=MESH,
        )

    token_swap = far_copy(tokens, far_tokens, 0)
    token_swap.start()

    def go(source, slot_id, own, send, recv):
        own.start()
        for c in range(CHUNKS):

            @pl.loop(1 if c == 0 else 0, per)
            def _(i):
                peer, mine, _ = mate(c, i, 1)
                pltpu.make_async_remote_copy(
                    src_ref=source.at[peer],
                    dst_ref=gathered.at[c, slot_id, mine],
                    send_sem=send.at[c],
                    recv_sem=recv.at[c],
                    device_id={"ep": peer},
                    device_id_type=MESH,
                ).start()

    own_go = pltpu.make_async_copy(outgoing.at[me], gathered.at[0, 0, seat], own_sem.at[0])
    go(outgoing, 0, own_go, go_send, go_recv)
    far_slot = n_tp - 1
    own_far_go = pltpu.make_async_copy(
        far_outgoing.at[me], gathered.at[0, far_slot, seat], own_sem.at[2]
    )

    def far_dispatch():
        token_swap.wait_recv()
        place_tokens(far_tokens, far_outgoing)
        go(far_outgoing, far_slot, own_far_go, far_go_send, far_go_recv)

    def all_bytes(c, source, target, send, recv):
        n = per - 1 if c == 0 else per
        if n == 0:
            return None
        return pltpu.make_async_remote_copy(
            src_ref=source.at[pl.ds(0, n)],
            dst_ref=target.at[pl.ds(0, n)],
            send_sem=send.at[c],
            recv_sem=recv.at[c],
            device_id={"tp": right},
            device_id_type=MESH,
        )

    def go_bytes(c):
        return all_bytes(c, outgoing, gathered.at[c, 0], go_send, go_recv)

    def far_go_bytes(c):
        return all_bytes(c, far_outgoing, gathered.at[c, far_slot], far_go_send, far_go_recv)

    def back_bytes(c):
        return all_bytes(c, answer.at[c], returned, back_send, back_recv)

    def far_back_bytes(c):
        return all_bytes(c, far_answer.at[c], far_returned, far_back_send, far_back_recv)

    def pass_on(c, source, slot_id, neighbour):
        return pltpu.make_async_remote_copy(
            src_ref=gathered.at[c, source],
            dst_ref=gathered.at[c, slot_id],
            send_sem=ag_send.at[c, slot_id],
            recv_sem=ag_recv.at[c, slot_id],
            device_id={"tp": neighbour},
            device_id_type=MESH,
        )

    def multiply(c, slot_id, origin):
        value = gathered[c, slot_id].astype(jnp.float32).reshape(many, features)
        return jnp.dot(
            value.astype(jnp.bfloat16), w_in[origin], preferred_element_type=jnp.float32
        )

    gather_copies, ring_copies = [], []

    def gather_begin(c):
        to_right, to_left = hops, hops
        if c == 0:
            own_go.wait()
        arrived = go_bytes(c)
        if arrived is not None:
            arrived.wait_recv()
        for length, slot_id, neighbour in ((to_right, 1, right), (to_left, to_right + 1, left)):
            if length > 0:
                copy = pass_on(c, 0, slot_id, neighbour)
                copy.start()
                gather_copies.append(copy)
        if c == 0:
            weight_copies[0].wait()
            weight_copies[1].wait()
        total[c] = multiply(c, 0, place)

    def gather_hop(c, j):
        to_right, to_left = hops, hops
        todo = []
        for length, base, neighbour, step in (
            (to_right, 0, right, n_tp - j),
            (to_left, to_right, left, j),
        ):
            if j <= length:
                pass_on(c, 0, base + j, neighbour).wait_recv()
                if j < length:
                    copy = pass_on(c, base + j, base + j + 1, neighbour)
                    copy.start()
                    gather_copies.append(copy)
                todo.append((base + j, lax.rem(place + step, n_tp)))
        for slot_id, origin in todo:
            total[c] += multiply(c, slot_id, origin)

    def far_gather(c):
        if c == 0:
            own_far_go.wait()
        arrived = far_go_bytes(c)
        if arrived is not None:
            arrived.wait_recv()
        total[c] += multiply(c, far_slot, opposite)

    def activate(c):
        gate, up = total[c, :, :units], total[c, :, units:]
        hidden[c] = (gate / (1.0 + jnp.exp(-gate)) * up).astype(jnp.bfloat16)

    def part(c, target):
        return jnp.dot(hidden[c], w_out[target], preferred_element_type=jnp.float32)

    def ring(c, j, to_right):
        sums, got, send, recv, neighbour = (
            (sum_right, got_right, right_send, right_recv, right)
            if to_right
            else (sum_left, got_left, left_send, left_recv, left)
        )
        return pltpu.make_async_remote_copy(
            src_ref=sums.at[c, j],
            dst_ref=got.at[c, j],
            send_sem=send.at[c, j],
            recv_sem=recv.at[c, j],
            device_id={"tp": neighbour},
            device_id_type=MESH,
        )

    def reduce_step(c, j):
        if j == 0:
            if c == 0:
                for copy in weight_copies[2:]:
                    copy.wait()
            activate(c)
        for length, to_right in ((hops, True), (hops, False)):
            if j < length:
                ahead = length - j if to_right else n_tp - (length - j)
                value = part(c, lax.rem(place + ahead, n_tp))
                sums, got = (sum_right, got_right) if to_right else (sum_left, got_left)
                if j > 0:
                    ring(c, j - 1, to_right).wait_recv()
                    value += got[c, j - 1].astype(jnp.float32)
                sums[c, j] = value.astype(jnp.bfloat16)
                copy = ring(c, j, to_right)
                copy.start()
                ring_copies.append(copy)

    def back(c, source, target, own, send, recv):
        if c == 0:
            own.start()

        @pl.loop(1 if c == 0 else 0, per)
        def _(i):
            peer, _, theirs = mate(c, i, -1)
            pltpu.make_async_remote_copy(
                src_ref=source.at[c, theirs],
                dst_ref=target.at[me],
                send_sem=send.at[c],
                recv_sem=recv.at[c],
                device_id={"ep": peer},
                device_id_type=MESH,
            ).start()

    own_back = pltpu.make_async_copy(answer.at[0, seat], returned.at[me], own_sem.at[1])
    own_far_back = pltpu.make_async_copy(
        far_answer.at[0, seat], far_returned.at[me], own_sem.at[3]
    )

    def far_reduce(c):
        value = part(c, opposite)
        far_answer[c] = value.reshape(per, rows, features).astype(jnp.bfloat16)
        back(c, far_answer, far_returned, own_far_back, far_back_send, far_back_recv)

    def reduce_end(c):
        value = part(c, place)
        for length, to_right in ((hops, True), (hops, False)):
            if length > 0:
                ring(c, length - 1, to_right).wait_recv()
                got = got_right if to_right else got_left
                value += got[c, length - 1].astype(jnp.float32)
        answer[c] = value.reshape(per, rows, features).astype(jnp.bfloat16)
        back(c, answer, returned, own_back, back_send, back_recv)

    events = [(FAR_AT, -1, far_dispatch)]
    for c in range(CHUNKS):
        start = OFFSETS[c]
        events.append((start, c, functools.partial(gather_begin, c)))
        for j in range(1, hops + 1):
            events.append((start + j, c, functools.partial(gather_hop, c, j)))
        events.append((start + hops, c, functools.partial(far_gather, c)))
        start += hops + 1
        for j in range(hops):
            events.append((start + j, c, functools.partial(reduce_step, c, j)))
        events.append((start, c, functools.partial(far_reduce, c)))
        events.append((start + hops, c, functools.partial(reduce_end, c)))
    for _, _, run in sorted(events, key=lambda event: event[:2]):
        run()

    scale = combine[...]
    high = scale.astype(jnp.bfloat16)
    low = (scale - high.astype(jnp.float32)).astype(jnp.bfloat16)

    def mix(source, own, arrivals):
        own.wait()
        for c in range(CHUNKS):
            arrived = arrivals(c)
            if arrived is not None:
                arrived.wait_recv()
        values = source[...].astype(jnp.float32).reshape(slots, features).astype(jnp.bfloat16)
        mixed = jnp.dot(high, values, preferred_element_type=jnp.float32)
        return mixed + jnp.dot(low, values, preferred_element_type=jnp.float32)

    far_mixed[...] = mix(far_returned, own_far_back, far_back_bytes)
    mixed_swap = far_copy(far_mixed, far_got, 1)
    mixed_swap.start()
    mixed = mix(returned, own_back, back_bytes)
    mixed_swap.wait_recv()
    out[...] = (mixed + far_got[...]).astype(jnp.bfloat16)

    for c in range(CHUNKS):
        for sent in (go_bytes(c), far_go_bytes(c), back_bytes(c), far_back_bytes(c)):
            if sent is not None:
                sent.wait_send()
    for copy in gather_copies + ring_copies + [token_swap, mixed_swap]:
        copy.wait_send()


def shards(tokens, routes, route_weight, w_gate, w_up, w_down):
    n_ep, n_tp = lax.axis_size("ep"), lax.axis_size("tp")
    batches, tok_rows, features = tokens.shape
    top = routes.shape[2]
    cap = 2 * tok_rows * top // n_ep
    toks, rows = batches * tok_rows, batches * cap
    units = w_gate.shape[2]
    per = n_ep // CHUNKS
    many = per * rows
    hops = n_tp // 2 - 1
    dma = pltpu.SemaphoreType.DMA
    vmem = pl.BlockSpec(memory_space=pltpu.VMEM)
    hbm = pl.BlockSpec(memory_space=pltpu.HBM)
    bf16, f32 = jnp.bfloat16, jnp.float32
    ring = pltpu.VMEM((CHUNKS, hops, many, features), bf16)
    out = pl.pallas_call(
        functools.partial(kernel, n_ep, n_tp, batches, cap),
        out_shape=jax.ShapeDtypeStruct((toks, features), bf16),
        in_specs=[hbm] * 6,
        out_specs=vmem,
        scratch_shapes=[
            pltpu.VMEM((batches, top, tok_rows), jnp.int32),
            pltpu.VMEM((batches, top, tok_rows), f32),
            pltpu.VMEM((toks, features), bf16),
            pltpu.VMEM((n_ep, rows, features), bf16),
            pltpu.VMEM((CHUNKS, n_tp, per, rows, features), bf16),
            pltpu.VMEM((toks, n_ep * rows), f32),
            pltpu.VMEM((n_tp, features, 2 * units), bf16),
            pltpu.VMEM((n_tp, units, features), bf16),
            pltpu.VMEM((CHUNKS, many, 2 * units), f32),
            pltpu.VMEM((CHUNKS, many, units), bf16),
            ring,
            ring,
            ring,
            ring,
            pltpu.VMEM((CHUNKS, per, rows, features), bf16),
            pltpu.VMEM((n_ep, rows, features), bf16),
            pltpu.VMEM((toks, features), bf16),
            pltpu.VMEM((n_ep, rows, features), bf16),
            pltpu.VMEM((CHUNKS, per, rows, features), bf16),
            pltpu.VMEM((n_ep, rows, features), bf16),
            pltpu.VMEM((toks, features), f32),
            pltpu.VMEM((toks, features), f32),
            dma((3,)),
            dma((4,)),
            dma((2 + n_tp,)),
            dma((CHUNKS,)),
            dma((CHUNKS,)),
            dma((CHUNKS, n_tp)),
            dma((CHUNKS, n_tp)),
            dma((CHUNKS, hops)),
            dma((CHUNKS, hops)),
            dma((CHUNKS, hops)),
            dma((CHUNKS, hops)),
            dma((CHUNKS,)),
            dma((CHUNKS,)),
            dma((2,)),
            dma((2,)),
            dma((CHUNKS,)),
            dma((CHUNKS,)),
            dma((CHUNKS,)),
            dma((CHUNKS,)),
        ],
        compiler_params=pltpu.CompilerParams(
            collective_id=0, has_side_effects=True, vmem_limit_bytes=67_043_328
        ),
        name="expert_layer",
    )(
        routes.swapaxes(1, 2),
        route_weight.swapaxes(1, 2),
        tokens.reshape(toks, features),
        w_gate.reshape(n_tp, features, units),
        w_up.reshape(n_tp, features, units),
        w_down.reshape(units, n_tp * features),
    )
    return out.reshape(batches, tok_rows, features)


def solution(mesh):
    return jax.shard_map(
        shards,
        mesh=mesh,
        in_specs=(
            P(None, "ep", "tp"),
            P(None, "ep", None),
            P(None, "ep", None),
            P("ep", None, "tp"),
            P("ep", None, "tp"),
            P("ep", "tp", None),
        ),
        out_specs=P(None, "ep", "tp"),
        check_vma=False,
    )
```

```python
import functools

import jax
import jax.numpy as jnp
from jax import lax
from jax.experimental import pallas as pl
from jax.experimental.pallas import tpu as pltpu
from jax.sharding import PartitionSpec as P

MESH = pl.DeviceIdType.MESH
DISTANCES = ((0,), (1,), (4,), (-3,), (3,), (-2,), (2,), (-1,))
DEPTH = 8
CORES = 2
CHUNKS = len(DISTANCES)
OFFSETS = (0, 0.34, 0.67, 1, 1.34, 1.67, 2, 2.34)
FAR_AT = 1.2


def log2(n):
    return n.bit_length() - 1


def kernel(
    n_ep, n_tp, batches, cap,
    routes_in, gains_in, tokens_in, w_gate, w_up, w_down, out,
    routes, weights, tokens, outgoing, gathered, combine, w_in, w_out, total, hidden,
    sum_right, sum_left, got_right, got_left, answer, returned,
    far_tokens, far_outgoing, far_answer, far_returned, far_mixed, far_got,
    in_sem, own_sem, w_sem, go_send, go_recv, ag_send, ag_recv,
    right_send, right_recv, left_send, left_recv, back_send, back_recv,
    far_send, far_recv, far_go_send, far_go_recv, far_back_send, far_back_recv,
):
    me = lax.axis_index("ep")
    place = lax.axis_index("tp")
    right, left = lax.rem(place + 1, n_tp), lax.rem(place + n_tp - 1, n_tp)
    opposite = lax.rem(place + n_tp // 2, n_tp)
    hops = n_tp // 2 - 1
    per = n_ep // CHUNKS
    core, z = lax.rem(me, CORES), lax.rem(lax.div(me, CORES), DEPTH)
    x = lax.div(me, CORES * DEPTH)
    layers = n_ep // DEPTH
    layer = x * CORES + core
    width = DEPTH // CHUNKS
    seat = layer * width

    def mate(c, i, sign):
        steps = DISTANCES[c]
        other = lax.rem(layer + lax.div(i, width), layers)
        q = lax.rem(i, width)
        far = steps[0] + q * (steps[-1] - steps[0])
        deep = lax.rem(z + sign * far + DEPTH, DEPTH)
        peer = (lax.div(other, CORES) * DEPTH + deep) * CORES + lax.rem(other, CORES)
        return peer, seat + q, other * width + q

    top, toks = routes.shape[1], tokens.shape[0]
    rows = batches * cap
    slots = n_ep * rows
    features = tokens.shape[1]
    units = w_gate.shape[2]
    many = per * rows

    small_copies = [
        pltpu.make_async_copy(source, target, in_sem.at[i])
        for i, (source, target) in enumerate(
            ((routes_in, routes), (gains_in, weights), (tokens_in, tokens))
        )
    ]
    for copy in small_copies:
        copy.start()

    weight_copies = [
        pltpu.make_async_copy(w_gate, w_in.at[:, :, pl.ds(0, units)], w_sem.at[0]),
        pltpu.make_async_copy(w_up, w_in.at[:, :, pl.ds(units, units)], w_sem.at[1]),
    ] + [
        pltpu.make_async_copy(
            w_down.at[:, pl.ds(g * features, features)], w_out.at[g], w_sem.at[2 + g]
        )
        for g in range(n_tp)
    ]
    for copy in weight_copies:
        copy.start()

    barrier = pltpu.get_barrier_semaphore()

    @pl.loop(1, n_ep)
    def _(i):
        pl.semaphore_signal(
            barrier, inc=1, device_id={"ep": lax.rem(me + i, n_ep)}, device_id_type=MESH
        )

    neighbours = (left, right, opposite)
    for neighbour in neighbours:
        pl.semaphore_signal(barrier, inc=1, device_id={"tp": neighbour}, device_id_type=MESH)

    for copy in small_copies:
        copy.wait()
    token = lax.broadcasted_iota(jnp.int32, (toks, slots), 0)
    slot = lax.broadcasted_iota(jnp.int32, (toks, slots), 1)
    expert = slot >> log2(rows)
    hits = jnp.zeros((toks, slots), jnp.float32)
    gains = jnp.zeros((toks, slots), jnp.float32)
    chosen = jnp.concatenate([routes[b].T for b in range(batches)], axis=0)
    factor = jnp.concatenate([weights[b].T for b in range(batches)], axis=0)
    for k in range(top):
        match = chosen[:, k : k + 1] == expert
        hits += jnp.where(match, 1.0, 0.0)
        gains += jnp.where(match, factor[:, k : k + 1], 0.0)
    block = log2(toks // batches)
    first = lax.broadcasted_iota(jnp.int32, (toks, toks), 0)
    second = lax.broadcasted_iota(jnp.int32, (toks, toks), 1)
    earlier = jnp.where(
        (second < first) & ((first >> block) == (second >> block)), 1.0, 0.0
    ).astype(jnp.bfloat16)
    rank = jnp.dot(earlier, hits.astype(jnp.bfloat16), preferred_element_type=jnp.float32)
    wanted = (slot & (cap - 1)).astype(jnp.float32)
    same = ((slot & (rows - 1)) >> log2(cap)) == (token >> block)
    picked = jnp.where((rank == wanted) & same, hits, 0.0)
    combine[...] = picked * gains
    def place_tokens(source, target):
        rows_out = lax.dot_general(
            picked.astype(jnp.bfloat16),
            source[...],
            (((0,), (0,)), ((), ())),
            preferred_element_type=jnp.float32,
        )
        target[...] = rows_out.reshape(n_ep, rows, features).astype(jnp.bfloat16)

    place_tokens(tokens, outgoing)

    pl.semaphore_wait(barrier, n_ep - 1 + len(neighbours))

    def far_copy(source, target, i):
        return pltpu.make_async_remote_copy(
            src_ref=source,
            dst_ref=target,
            send_sem=far_send.at[i],
            recv_sem=far_recv.at[i],
            device_id={"tp": opposite},
            device_id_type=MESH,
        )

    token_swap = far_copy(tokens, far_tokens, 0)
    token_swap.start()

    def go(source, slot_id, own, send, recv):
        own.start()
        for c in range(CHUNKS):

            @pl.loop(1 if c == 0 else 0, per)
            def _(i):
                peer, mine, _ = mate(c, i, 1)
                pltpu.make_async_remote_copy(
                    src_ref=source.at[peer],
                    dst_ref=gathered.at[c, slot_id, mine],
                    send_sem=send.at[c],
                    recv_sem=recv.at[c],
                    device_id={"ep": peer},
                    device_id_type=MESH,
                ).start()

    own_go = pltpu.make_async_copy(outgoing.at[me], gathered.at[0, 0, seat], own_sem.at[0])
    go(outgoing, 0, own_go, go_send, go_recv)
    far_slot = n_tp - 1
    own_far_go = pltpu.make_async_copy(
        far_outgoing.at[me], gathered.at[0, far_slot, seat], own_sem.at[2]
    )

    def far_dispatch():
        token_swap.wait_recv()
        place_tokens(far_tokens, far_outgoing)
        go(far_outgoing, far_slot, own_far_go, far_go_send, far_go_recv)

    def all_bytes(c, source, target, send, recv):
        n = per - 1 if c == 0 else per
        if n == 0:
            return None
        return pltpu.make_async_remote_copy(
            src_ref=source.at[pl.ds(0, n)],
            dst_ref=target.at[pl.ds(0, n)],
            send_sem=send.at[c],
            recv_sem=recv.at[c],
            device_id={"tp": right},
            device_id_type=MESH,
        )

    def go_bytes(c):
        return all_bytes(c, outgoing, gathered.at[c, 0], go_send, go_recv)

    def far_go_bytes(c):
        return all_bytes(c, far_outgoing, gathered.at[c, far_slot], far_go_send, far_go_recv)

    def back_bytes(c):
        return all_bytes(c, answer.at[c], returned, back_send, back_recv)

    def far_back_bytes(c):
        return all_bytes(c, far_answer.at[c], far_returned, far_back_send, far_back_recv)

    def pass_on(c, source, slot_id, neighbour):
        return pltpu.make_async_remote_copy(
            src_ref=gathered.at[c, source],
            dst_ref=gathered.at[c, slot_id],
            send_sem=ag_send.at[c, slot_id],
            recv_sem=ag_recv.at[c, slot_id],
            device_id={"tp": neighbour},
            device_id_type=MESH,
        )

    def multiply(c, slot_id, origin):
        value = gathered[c, slot_id].astype(jnp.float32).reshape(many, features)
        return jnp.dot(
            value.astype(jnp.bfloat16), w_in[origin], preferred_element_type=jnp.float32
        )

    gather_copies, ring_copies = [], []

    def gather_begin(c):
        to_right, to_left = hops, hops
        if c == 0:
            own_go.wait()
        arrived = go_bytes(c)
        if arrived is not None:
            arrived.wait_recv()
        for length, slot_id, neighbour in ((to_right, 1, right), (to_left, to_right + 1, left)):
            if length > 0:
                copy = pass_on(c, 0, slot_id, neighbour)
                copy.start()
                gather_copies.append(copy)
        if c == 0:
            weight_copies[0].wait()
            weight_copies[1].wait()
        total[c] = multiply(c, 0, place)

    def gather_hop(c, j):
        to_right, to_left = hops, hops
        todo = []
        for length, base, neighbour, step in (
            (to_right, 0, right, n_tp - j),
            (to_left, to_right, left, j),
        ):
            if j <= length:
                pass_on(c, 0, base + j, neighbour).wait_recv()
                if j < length:
                    copy = pass_on(c, base + j, base + j + 1, neighbour)
                    copy.start()
                    gather_copies.append(copy)
                todo.append((base + j, lax.rem(place + step, n_tp)))
        for slot_id, origin in todo:
            total[c] += multiply(c, slot_id, origin)

    def far_gather(c):
        if c == 0:
            own_far_go.wait()
        arrived = far_go_bytes(c)
        if arrived is not None:
            arrived.wait_recv()
        total[c] += multiply(c, far_slot, opposite)

    def activate(c):
        gate, up = total[c, :, :units], total[c, :, units:]
        hidden[c] = (gate / (1.0 + jnp.exp(-gate)) * up).astype(jnp.bfloat16)

    def part(c, target):
        return jnp.dot(hidden[c], w_out[target], preferred_element_type=jnp.float32)

    def ring(c, j, to_right):
        sums, got, send, recv, neighbour = (
            (sum_right, got_right, right_send, right_recv, right)
            if to_right
            else (sum_left, got_left, left_send, left_recv, left)
        )
        return pltpu.make_async_remote_copy(
            src_ref=sums.at[c, j],
            dst_ref=got.at[c, j],
            send_sem=send.at[c, j],
            recv_sem=recv.at[c, j],
            device_id={"tp": neighbour},
            device_id_type=MESH,
        )

    def reduce_step(c, j):
        if j == 0:
            if c == 0:
                for copy in weight_copies[2:]:
                    copy.wait()
            activate(c)
        for length, to_right in ((hops, True), (hops, False)):
            if j < length:
                ahead = length - j if to_right else n_tp - (length - j)
                value = part(c, lax.rem(place + ahead, n_tp))
                sums, got = (sum_right, got_right) if to_right else (sum_left, got_left)
                if j > 0:
                    ring(c, j - 1, to_right).wait_recv()
                    value += got[c, j - 1].astype(jnp.float32)
                sums[c, j] = value.astype(jnp.bfloat16)
                copy = ring(c, j, to_right)
                copy.start()
                ring_copies.append(copy)

    def back(c, source, target, own, send, recv):
        if c == 0:
            own.start()

        @pl.loop(1 if c == 0 else 0, per)
        def _(i):
            peer, _, theirs = mate(c, i, -1)
            pltpu.make_async_remote_copy(
                src_ref=source.at[c, theirs],
                dst_ref=target.at[me],
                send_sem=send.at[c],
                recv_sem=recv.at[c],
                device_id={"ep": peer},
                device_id_type=MESH,
            ).start()

    own_back = pltpu.make_async_copy(answer.at[0, seat], returned.at[me], own_sem.at[1])
    own_far_back = pltpu.make_async_copy(
        far_answer.at[0, seat], far_returned.at[me], own_sem.at[3]
    )

    def far_reduce(c):
        value = part(c, opposite)
        far_answer[c] = value.reshape(per, rows, features).astype(jnp.bfloat16)
        back(c, far_answer, far_returned, own_far_back, far_back_send, far_back_recv)

    def reduce_end(c):
        value = part(c, place)
        for length, to_right in ((hops, True), (hops, False)):
            if length > 0:
                ring(c, length - 1, to_right).wait_recv()
                got = got_right if to_right else got_left
                value += got[c, length - 1].astype(jnp.float32)
        answer[c] = value.reshape(per, rows, features).astype(jnp.bfloat16)
        back(c, answer, returned, own_back, back_send, back_recv)

    events = [(FAR_AT, -1, far_dispatch)]
    for c in range(CHUNKS):
        start = OFFSETS[c]
        events.append((start, c, functools.partial(gather_begin, c)))
        for j in range(1, hops + 1):
            events.append((start + j, c, functools.partial(gather_hop, c, j)))
        events.append((start + hops, c, functools.partial(far_gather, c)))
        start += hops + 1
        for j in range(hops):
            events.append((start + j, c, functools.partial(reduce_step, c, j)))
        events.append((start, c, functools.partial(far_reduce, c)))
        events.append((start + hops, c, functools.partial(reduce_end, c)))
    for _, _, run in sorted(events, key=lambda event: event[:2]):
        run()

    scale = combine[...]
    high = scale.astype(jnp.bfloat16)
    low = (scale - high.astype(jnp.float32)).astype(jnp.bfloat16)

    def mix(source, own, arrivals):
        own.wait()
        for c in range(CHUNKS):
            arrived = arrivals(c)
            if arrived is not None:
                arrived.wait_recv()
        values = source[...].astype(jnp.float32).reshape(slots, features).astype(jnp.bfloat16)
        mixed = jnp.dot(high, values, preferred_element_type=jnp.float32)
        return mixed + jnp.dot(low, values, preferred_element_type=jnp.float32)

    far_mixed[...] = mix(far_returned, own_far_back, far_back_bytes)
    mixed_swap = far_copy(far_mixed, far_got, 1)
    mixed_swap.start()
    mixed = mix(returned, own_back, back_bytes)
    mixed_swap.wait_recv()
    out[...] = (mixed + far_got[...]).astype(jnp.bfloat16)

    for c in range(CHUNKS):
        for sent in (go_bytes(c), far_go_bytes(c), back_bytes(c), far_back_bytes(c)):
            if sent is not None:
                sent.wait_send()
    for copy in gather_copies + ring_copies + [token_swap, mixed_swap]:
        copy.wait_send()


def shards(tokens, routes, route_weight, w_gate, w_up, w_down):
    n_ep, n_tp = lax.axis_size("ep"), lax.axis_size("tp")
    batches, tok_rows, features = tokens.shape
    top = routes.shape[2]
    cap = 2 * tok_rows * top // n_ep
    toks, rows = batches * tok_rows, batches * cap
    units = w_gate.shape[2]
    per = n_ep // CHUNKS
    many = per * rows
    hops = n_tp // 2 - 1
    dma = pltpu.SemaphoreType.DMA
    vmem = pl.BlockSpec(memory_space=pltpu.VMEM)
    hbm = pl.BlockSpec(memory_space=pltpu.HBM)
    bf16, f32 = jnp.bfloat16, jnp.float32
    ring = pltpu.VMEM((CHUNKS, hops, many, features), bf16)
    out = pl.pallas_call(
        functools.partial(kernel, n_ep, n_tp, batches, cap),
        out_shape=jax.ShapeDtypeStruct((toks, features), bf16),
        in_specs=[hbm] * 6,
        out_specs=vmem,
        scratch_shapes=[
            pltpu.VMEM((batches, top, tok_rows), jnp.int32),
            pltpu.VMEM((batches, top, tok_rows), f32),
            pltpu.VMEM((toks, features), bf16),
            pltpu.VMEM((n_ep, rows, features), bf16),
            pltpu.VMEM((CHUNKS, n_tp, per, rows, features), bf16),
            pltpu.VMEM((toks, n_ep * rows), f32),
            pltpu.VMEM((n_tp, features, 2 * units), bf16),
            pltpu.VMEM((n_tp, units, features), bf16),
            pltpu.VMEM((CHUNKS, many, 2 * units), f32),
            pltpu.VMEM((CHUNKS, many, units), bf16),
            ring,
            ring,
            ring,
            ring,
            pltpu.VMEM((CHUNKS, per, rows, features), bf16),
            pltpu.VMEM((n_ep, rows, features), bf16),
            pltpu.VMEM((toks, features), bf16),
            pltpu.VMEM((n_ep, rows, features), bf16),
            pltpu.VMEM((CHUNKS, per, rows, features), bf16),
            pltpu.VMEM((n_ep, rows, features), bf16),
            pltpu.VMEM((toks, features), f32),
            pltpu.VMEM((toks, features), f32),
            dma((3,)),
            dma((4,)),
            dma((2 + n_tp,)),
            dma((CHUNKS,)),
            dma((CHUNKS,)),
            dma((CHUNKS, n_tp)),
            dma((CHUNKS, n_tp)),
            dma((CHUNKS, hops)),
            dma((CHUNKS, hops)),
            dma((CHUNKS, hops)),
            dma((CHUNKS, hops)),
            dma((CHUNKS,)),
            dma((CHUNKS,)),
            dma((2,)),
            dma((2,)),
            dma((CHUNKS,)),
            dma((CHUNKS,)),
            dma((CHUNKS,)),
            dma((CHUNKS,)),
        ],
        compiler_params=pltpu.CompilerParams(
            collective_id=0, has_side_effects=True, vmem_limit_bytes=67_043_328
        ),
        name="expert_layer",
    )(
        routes.swapaxes(1, 2),
        route_weight.swapaxes(1, 2),
        tokens.reshape(toks, features),
        w_gate.reshape(n_tp, features, units),
        w_up.reshape(n_tp, features, units),
        w_down.reshape(units, n_tp * features),
    )
    return out.reshape(batches, tok_rows, features)


def solution(mesh):
    return jax.shard_map(
        shards,
        mesh=mesh,
        in_specs=(
            P(None, "ep", "tp"),
            P(None, "ep", None),
            P(None, "ep", None),
            P("ep", None, "tp"),
            P("ep", None, "tp"),
            P("ep", "tp", None),
        ),
        out_specs=P(None, "ep", "tp"),
        check_vma=False,
    )
```
